256 devices in a mesh: grp: 8 (over z_lo, y), sub: 32 (over z_hi, x, core).
Axes of the slice: x: 4, y: 4, z: 8 (z_hi: 4, z_lo: 2; z = z_hi * 2 + z_lo), core: 2. Of those that a mesh axis runs over, the one named last changes fastest.
Arguments:
- right_side: float32 [16, 128, 512, 128], P(None, 'grp', 'sub'), may hold values from -12 to 12
- conductivity: float32 [128, 512, 128], P('grp', 'sub'), may hold values from 0.1 to 10
- pinned_cells: int32 [128, 512, 128], P('grp', 'sub'), may hold values 0 or 1
- coarse_basis: float32 [32, 128, 512, 128], P(None, 'grp', 'sub'), may hold values from -0.03125 to 0.03125
- coarse_inverse: float32 [8, 1024, 8192], P(None, 'sub', 'grp'), as said below
Outputs:
- solution: float32 [16, 128, 512, 128], P(None, 'grp', 'sub')
- residual: float32 [16, 128, 512, 128], P(None, 'grp', 'sub')
The draws below stay inside these ranges and needn't reach their ends.
Inputs may be any that keep to these rules, and one draw needn't show every extreme that they name: coarse_inverse is symmetric as a 8192 x 8192 matrix.
All inputs are finite; a program needn't handle non-finite values. No bound on the sum of `pinned_cells` on one device may be relied on, other than what follows from the above.
Results may differ from the reference program's by a relative error of at most 0.0003.
Values sent between devices are 32-bit elements; how exact they have to be, the bound alone decides.
No kernel may reach another device: no remote copies, remote signals or barrier semaphores. Data moves between devices by JAX's collectives and lax.ppermute only.
A program may use at most 128 MiB of HBM per device.

```python
import math
import jax
import jax.numpy as jnp
from jax import lax

CX = 16
CY = 16
CZ = 128
SOURCES = 16
VECTORS = 32
ITERS = 2
NX = 128
NY = 512
NZ = 128
GROUP_DOFS = 1024
COARSE = 8192
N_GRP = 8
N_SUB = 32


def draw_right_side(key, part):
    field_shape = (SOURCES, NX, NY, NZ)
    row_index = jnp.arange(NX, dtype=jnp.float32)[:, None]
    col_index = jnp.arange(NY, dtype=jnp.float32)[None, :]
    rising = 1.0 + 2.0 * (row_index * NY + col_index) / (NX * NY)
    rising = rising[None, :, :, None]
    values = 1.5 * rising * jax.random.normal(key, field_shape, jnp.float32)
    return jnp.clip(values, -12.0, 12.0)


def draw_coarse_inverse(key, part):
    magnitude = 0.07 * math.sqrt(CX * CY * CZ // VECTORS)
    entries = jnp.clip(jax.random.normal(key, (COARSE, COARSE), jnp.float32), -4.0, 4.0)
    symmetric = (entries + entries.T) * (0.45 / math.sqrt(2.0 * COARSE))
    identity = jnp.eye(COARSE, dtype=jnp.float32)
    matrix = magnitude * (symmetric * (1.0 - identity) + 1.5 * identity)
    return matrix.reshape(COARSE // GROUP_DOFS, GROUP_DOFS, COARSE)


def touch_ends(array, own_key, least, top_value):
    place = [jax.random.randint(jax.random.fold_in(own_key, axis), (), 0, length) for axis, length in enumerate(array.shape)]
    main_axis = array.shape.index(max(array.shape))
    neighbour = place[:main_axis] + [(place[main_axis] + 1) % array.shape[main_axis]] + place[main_axis + 1:]
    return array.at[tuple(place)].set(least).at[tuple(neighbour)].set(top_value)


def levels(stream_key, shape, cuts, low, largest):
    def one(dim, blocks):
        draws = jax.random.uniform(jax.random.fold_in(jax.random.fold_in(stream_key, 6), dim), (blocks,), jnp.float32, low / len(cuts), largest / len(cuts))
        return jnp.repeat(jnp.exp(draws), shape[dim] // blocks).reshape((-1,) + (1,) * (len(shape) - dim - 1))

    level = one(*cuts[0])
    for cut in cuts[1:]:
        level = level * one(*cut)
    return level


def scatter_about(rng, shape, spread, reach, split=(), kind=jnp.bfloat16):
    loudness = levels(rng, shape, split, -0.22, 0.18) if split else 1.0
    drawn = jax.random.normal(rng, shape, jnp.float32) * spread * loudness
    return jnp.minimum(jnp.maximum(drawn, -reach), reach).astype(kind)


def setup_inputs(seed: int = 0) -> dict:
    key_list = jax.random.split(jax.random.key(seed), 6)
    return {
        "right_side": draw_right_side(jax.random.fold_in(key_list[5], 71), 0),
        "conductivity": jnp.clip(jnp.exp(math.log(10.0) - 4.6051702 * jax.random.uniform(key_list[1], (NX, NY, NZ), jnp.float32) ** levels(key_list[1], (NX, NY, NZ), ((0, 8), (1, 32)), -0.2, 0.2)), 0.1, 10.0),
        "pinned_cells": touch_ends((jax.random.randint(key_list[2], (NX, NY, NZ), 0, 8) < 1).astype(jnp.int32), jax.random.fold_in(key_list[2], 1), 0, 1),
        "coarse_basis": scatter_about(key_list[3], (VECTORS, NX, NY, NZ), (CX * CY * CZ) ** -0.5, 0.03125, ((1, 8), (2, 32)), jnp.float32),
        "coarse_inverse": draw_coarse_inverse(jax.random.fold_in(key_list[5], 71), 0),
    }


def inner_product(left, right):
    return jnp.einsum('ixyz,jxyz->ij', left, right, precision=lax.Precision.HIGHEST)

def combine(field, coeffs):
    return jnp.einsum('ixyz,ij->jxyz', field, coeffs, precision=lax.Precision.HIGHEST)

def solve_spd(matrix, right):
    factor = jnp.linalg.cholesky(matrix)
    return jax.scipy.linalg.cho_solve((factor, True), right)

def face_weights(conductivity):
    padded = jnp.pad(conductivity, 1)
    faces_first = 0.5 * (padded[:-1, 1:-1, 1:-1] + padded[1:, 1:-1, 1:-1])
    faces_second = 0.5 * (padded[1:-1, :-1, 1:-1] + padded[1:-1, 1:, 1:-1])
    faces_third = 0.5 * (padded[1:-1, 1:-1, :-1] + padded[1:-1, 1:-1, 1:])
    centre = faces_first[1:] + faces_first[:-1] + faces_second[:, 1:] + faces_second[:, :-1]
    centre = centre + faces_third[:, :, 1:] + faces_third[:, :, :-1]
    return (faces_first, faces_second, faces_third, centre)

def operate(field, face_set, keeper, pinned):
    faces_first, faces_second, faces_third, centre = face_set
    masked = keeper * field
    padded = jnp.pad(masked, ((0, 0), (1, 1), (1, 1), (1, 1)))
    beside = faces_first[1:] * padded[:, 2:, 1:-1, 1:-1] + faces_first[:-1] * padded[:, :-2, 1:-1, 1:-1]
    beside = beside + faces_second[:, 1:] * padded[:, 1:-1, 2:, 1:-1] + faces_second[:, :-1] * padded[:, 1:-1, :-2, 1:-1]
    beside = beside + faces_third[:, :, 1:] * padded[:, 1:-1, 1:-1, 2:] + faces_third[:, :, :-1] * padded[:, 1:-1, 1:-1, :-2]
    return keeper * (centre * masked - beside) + pinned * field

def precondition(residual, coarse_basis, coarse_inverse, scaling):
    shaped_res = residual.reshape(SOURCES, N_GRP, CX, N_SUB, CY, NZ)
    shaped_basis = coarse_basis.reshape(VECTORS, N_GRP, CX, N_SUB, CY, NZ)

    def restrict_group(group_index):
        return jnp.einsum('kxsyz,jxsyz->skj', shaped_basis[:, group_index], shaped_res[:, group_index], precision=lax.Precision.HIGHEST)
    coeffs = lax.map(restrict_group, jnp.arange(N_GRP, dtype=jnp.int32))
    coeffs = coeffs.reshape(COARSE, SOURCES)
    matrix = coarse_inverse.reshape(COARSE, COARSE)
    answer = jnp.dot(matrix, coeffs, precision=lax.Precision.HIGHEST)
    answer = answer.reshape(N_GRP, N_SUB, VECTORS, SOURCES)

    def prolong_group(group_index):
        return jnp.einsum('kxsyz,skj->jxsyz', shaped_basis[:, group_index], answer[group_index], precision=lax.Precision.HIGHEST)
    coarse_part = lax.map(prolong_group, jnp.arange(N_GRP, dtype=jnp.int32))
    coarse_part = jnp.moveaxis(coarse_part, 0, 1).reshape(SOURCES, NX, NY, NZ)
    return scaling * residual + coarse_part

def reference(right_side, conductivity, pinned_cells, coarse_basis, coarse_inverse):
    face_set = face_weights(conductivity)
    pinned = pinned_cells.astype(jnp.float32)
    keeper = 1.0 - pinned
    scaling = 1.0 / (keeper * face_set[3] + pinned)
    solution = jnp.zeros_like(right_side)
    residual = right_side
    direction = precondition(residual, coarse_basis, coarse_inverse, scaling)
    image_field = operate(direction, face_set, keeper, pinned)
    for sweep_index in range(ITERS):
        curvature = inner_product(direction, image_field)
        projection = inner_product(direction, residual)
        weights = solve_spd(curvature, projection)
        solution = solution + combine(direction, weights)
        residual = residual - combine(image_field, weights)
        if sweep_index + 1 < ITERS:
            smoothed = precondition(residual, coarse_basis, coarse_inverse, scaling)
            coupling = inner_product(image_field, smoothed)
            mixing = -solve_spd(curvature, coupling)
            direction = smoothed + combine(direction, mixing)
            image_field = operate(direction, face_set, keeper, pinned)
    return (solution, residual)
```

```python
import functools

import jax
import jax.numpy as jnp
from jax import lax
from jax.sharding import Mesh
from jax.sharding import PartitionSpec as P

GRP = ("grp_0", "grp_1")
SUB = ("sub_0", "sub_1", "sub_2")


def extended(array, sides, width):
    edges = {}
    for axis, dim in sides:
        count, length = (lax.axis_size(axis), array.shape[dim])
        up = [(i, (i + 1) % count) for i in range(count - 1)]
        last = lax.slice_in_dim(array, length - width, length, axis=dim)
        first = lax.slice_in_dim(array, 0, width, axis=dim)
        edges[dim] = (
            lax.ppermute(last, axis, up),
            lax.ppermute(first, axis, [(b, a) for a, b in up]),
        )
    done = []
    for _, dim in sides:
        low, high = edges[dim]
        around = [(width, width) if d in done else (0, 0) for d in range(array.ndim)]
        array = jnp.concatenate([jnp.pad(low, around), array, jnp.pad(high, around)], axis=dim)
        done.append(dim)
    return array


def joined_along(pieces, dim):
    dims = list(pieces.shape[1:])
    dims[dim] *= pieces.shape[0]
    return jnp.moveaxis(pieces, 0, dim).reshape(dims)


def copy_for_each(array, axis):
    copies = jnp.broadcast_to(array, (lax.axis_size(axis), *array.shape))
    return lax.all_to_all(copies, axis, split_axis=0, concat_axis=0, tiled=True)


def gather_directly(array, axis, dim):
    return joined_along(copy_for_each(array, axis), dim)


def split_up(array, dim, count):
    before, after = (array.shape[:dim], array.shape[dim + 1 :])
    return jnp.moveaxis(array.reshape(*before, count, -1, *after), dim, 0)


def sum_at_owner(array, axis, dim):
    pieces = split_up(array, dim, lax.axis_size(axis))
    arrived = lax.all_to_all(pieces, axis, split_axis=0, concat_axis=0, tiled=True)
    return arrived.sum(axis=0)


def sum_over_all(array):
    for axes in (("grp_0", "grp_1", "sub_2"), ("sub_0", "sub_1")):
        array = copy_for_each(array, axes).sum(axis=0)
    return array


def inner_product(left, right):
    return jnp.einsum("ixyz,jxyz->ij", left, right, precision=lax.Precision.HIGHEST)


def combine(field, coeffs):
    return jnp.einsum("ixyz,ij->jxyz", field, coeffs, precision=lax.Precision.HIGHEST)


def small_product(left, right):
    return jnp.dot(left, right, precision=lax.Precision.HIGHEST)


def solve_spd(matrix, right):
    factor = jnp.linalg.cholesky(matrix)
    return jax.scipy.linalg.cho_solve((factor, True), right)


def face_weights(conductivity):
    padded = extended(conductivity, ((GRP, 0), (SUB, 1)), 1)
    faces_first = 0.5 * (padded[:-1, 1:-1] + padded[1:, 1:-1])
    faces_second = 0.5 * (padded[1:-1, :-1] + padded[1:-1, 1:])
    vertical = jnp.pad(conductivity, ((0, 0), (0, 0), (1, 1)))
    faces_third = 0.5 * (vertical[:, :, :-1] + vertical[:, :, 1:])
    centre = faces_first[1:] + faces_first[:-1] + faces_second[:, 1:] + faces_second[:, :-1]
    centre = centre + faces_third[:, :, 1:] + faces_third[:, :, :-1]
    return (faces_first, faces_second, faces_third, centre)


def operate(field, face_set, keeper, pinned):
    faces_first, faces_second, faces_third, centre = face_set
    masked = keeper * field
    padded = extended(masked, ((GRP, 1), (SUB, 2)), 1)
    vertical = jnp.pad(masked, ((0, 0), (0, 0), (0, 0), (1, 1)))
    beside = faces_first[1:] * padded[:, 2:, 1:-1] + faces_first[:-1] * padded[:, :-2, 1:-1]
    beside = (
        beside
        + faces_second[:, 1:] * padded[:, 1:-1, 2:]
        + faces_second[:, :-1] * padded[:, 1:-1, :-2]
    )
    beside = (
        beside
        + faces_third[:, :, 1:] * vertical[:, :, :, 2:]
        + faces_third[:, :, :-1] * vertical[:, :, :, :-2]
    )
    return keeper * (centre * masked - beside) + pinned * field


def precondition(residual, coarse_basis, coarse_inverse, scaling):
    local_coeffs = jnp.einsum(
        "kxyz,jxyz->kj", coarse_basis, residual, precision=lax.Precision.HIGHEST
    )
    group_coeffs = gather_directly(local_coeffs, SUB, 0)
    flat_rows = coarse_inverse.reshape(-1, coarse_inverse.shape[2])
    answer = sum_at_owner(
        jnp.dot(
            flat_rows,
            group_coeffs,
            precision=lax.Precision.HIGHEST,
            preferred_element_type=jnp.float32,
        ),
        GRP,
        0,
    )
    coarse_part = jnp.einsum("kxyz,kj->jxyz", coarse_basis, answer, precision=lax.Precision.HIGHEST)
    return scaling * residual + coarse_part


def local(right_side, conductivity, pinned_cells, coarse_basis, coarse_inverse):
    face_set = face_weights(conductivity)
    pinned = pinned_cells.astype(jnp.float32)
    keeper = 1.0 - pinned
    scaling = 1.0 / (keeper * face_set[3] + pinned)
    first = precondition(right_side, coarse_basis, coarse_inverse, scaling)
    first_image = operate(first, face_set, keeper, pinned)
    second = precondition(first_image, coarse_basis, coarse_inverse, scaling)
    second_image = operate(second, face_set, keeper, pinned)
    partial = jnp.stack(
        [
            inner_product(first, right_side),
            inner_product(first, first_image),
            inner_product(first_image, second),
            inner_product(second, second_image),
        ]
    )
    projection, curvature, cross, energy = sum_over_all(partial.reshape(8, 128)).reshape(4, 16, 16)
    both = solve_spd(curvature, jnp.concatenate([projection, cross], axis=1))
    weights, mix = both[:, :16], both[:, 16:]
    last = solve_spd(
        energy - small_product(cross.T, mix), small_product(cross.T, weights) - curvature
    )
    on_first = weights + small_product(mix, last)
    solution = combine(first, on_first) - combine(second, last)
    residual = right_side - combine(first_image, on_first) + combine(second_image, last)
    return (solution, residual)


def solution(mesh):
    split = Mesh(mesh.devices.reshape(2, 4, 4, 4, 2), ("grp_0", "grp_1", "sub_0", "sub_1", "sub_2"))
    in_specs = (
        P(None, GRP, SUB, None),
        P(GRP, SUB, None),
        P(GRP, SUB, None),
        P(None, GRP, SUB, None),
        P(None, SUB, GRP),
    )
    out_specs = (P(None, GRP, SUB, None), P(None, GRP, SUB, None))
    return jax.shard_map(local, mesh=split, in_specs=in_specs, out_specs=out_specs, check_vma=False)
```

```python
import jax
import jax.numpy as jnp
from jax import lax
from jax.experimental import pallas as pl
from jax.experimental.pallas import tpu as pltpu
from jax.sharding import Mesh
from jax.sharding import PartitionSpec as P

GRP = ("grp_0", "grp_1")
SUB = ("sub_0", "sub_1", "sub_2")
N_GRP, N_SUB = 8, 32
F32, BF16 = jnp.float32, jnp.bfloat16
HIGHEST = lax.Precision.HIGHEST
CX, CY, CZ, SRC, VEC = 16, 16, 128, 16, 32
FIELD = (SRC, CX, CY, CZ)


def iota(shape, dim):
    return lax.broadcasted_iota(jnp.int32, shape, dim)


def exact_dot(left, right):
    return jnp.dot(left, right, precision=HIGHEST, preferred_element_type=F32)


def split(value):
    high = value.astype(BF16)
    return high, (value - high.astype(F32)).astype(BF16)


def dot3(left, right, dims):
    (lh, ll), (rh, rl) = left, right

    def one(a, b):
        return lax.dot_general(a, b, (dims, ((), ())), preferred_element_type=F32)

    return one(lh, rh) + (one(lh, rl) + one(ll, rh))


ROWS_BY_ROWS = ((1,), (1,))
PLAIN = ((1,), (0,))


def slab(ref, x):
    count = ref.shape[0]
    halves = [ref[:, x, 8 * h : 8 * h + 8, :].reshape(count * 8, CZ) for h in range(2)]
    return jnp.concatenate(halves, axis=1)


def pack(total):
    rows = total.shape[0]
    same = iota(total.shape, 0) % 8 == iota(total.shape, 1) % 8
    summed = jnp.where(same, total, 0.0).reshape(rows // 8, 8, 128).sum(axis=1)
    spread = exact_dot(summed, (iota((128, 128), 0) // 8 == iota((128, 128), 1) % 16).astype(F32))
    mine = iota(spread.shape, 0) % 8 == iota(spread.shape, 1) // 16
    return jnp.where(mine, spread, 0.0).reshape(rows // 64, 8, 128).sum(axis=1)


def spread_rows(packed):
    count = packed.shape[0]
    pieces = [jnp.broadcast_to(packed[r : r + 1], (8, 128)) for r in range(count)]
    wide = jnp.concatenate(pieces, axis=0)
    return jnp.where(iota(wide.shape, 0) % 8 == iota(wide.shape, 1) // 16, wide, 0.0)


def unpack(packed, offset):
    pick = iota((128, 128), 0) % 16 == iota((128, 128), 1) - offset
    return exact_dot(spread_rows(packed), pick.astype(F32))


def kron_rows(values):
    count = values.shape[0]
    pieces = [jnp.broadcast_to(values[n : n + 1], (8, 128)) for n in range(count)]
    wide = jnp.concatenate(pieces, axis=0)
    return jnp.where(iota(wide.shape, 0) % 8 == iota(wide.shape, 1) % 8, wide, 0.0)


def put_copies(out_ref, value):
    for n in range(out_ref.shape[0]):
        out_ref[n] = value


def add_up(ref):
    total = ref[0]
    for n in range(1, ref.shape[0]):
        total = total + ref[n]
    return total


def faces_kernel(cond, pinned, x_lo, x_hi, y_lo, y_hi, scaling, keep, coef):
    g = lax.axis_index("grp_0") * 4 + lax.axis_index("grp_1")
    s = (lax.axis_index("sub_0") * 4 + lax.axis_index("sub_1")) * 2 + lax.axis_index("sub_2")

    def inside(count, flag):
        return jnp.broadcast_to(flag.astype(F32), (count, CZ))

    has_x_lo, has_x_hi = inside(CY, g > 0), inside(CY, g < N_GRP - 1)
    has_y_lo, has_y_hi = inside(1, s > 0), inside(1, s < N_SUB - 1)
    rows = iota((CY, CZ), 0)
    lanes = iota((CY, CZ), 1)

    def down(v, edge):
        return jnp.where(rows == 0, edge, pltpu.roll(v, 1, 0))

    def up(v, edge):
        return jnp.where(rows == CY - 1, edge, pltpu.roll(v, CY - 1, 0))

    def left(v):
        return jnp.where(lanes == 0, 0.0, pltpu.roll(v, 1, 1))

    def right(v):
        return jnp.where(lanes == CZ - 1, 0.0, pltpu.roll(v, CZ - 1, 1))

    for x in range(CX):
        keep[x] = 1.0 - pinned[x].astype(F32)
    for x in range(CX):
        c, k = cond[x], keep[x]
        c_lo = cond[x - 1] if x else has_x_lo * x_lo[...]
        c_hi = cond[x + 1] if x < CX - 1 else has_x_hi * x_hi[...]
        k_lo = keep[x - 1] if x else has_x_lo
        k_hi = keep[x + 1] if x < CX - 1 else has_x_hi
        beside = [
            (c_lo, k_lo),
            (c_hi, k_hi),
            (down(c, has_y_lo * y_lo[x : x + 1]), down(k, has_y_lo)),
            (up(c, has_y_hi * y_hi[x : x + 1]), up(k, has_y_hi)),
            (left(c), left(k)),
            (right(c), right(k)),
        ]
        centre = None
        for n, (other, mask) in enumerate(beside):
            face = 0.5 * (c + other)
            centre = face if centre is None else centre + face
            coef[n, x] = (k * mask) * face
        whole = k * centre + (1.0 - k)
        coef[6, x] = whole
        scaling[x] = 1.0 / whole


def restrict_kernel(basis, field, out, total):
    total[...] = jnp.zeros_like(total)

    def step(x, carry):
        total[...] += dot3(split(slab(basis, x)), split(slab(field, x)), ROWS_BY_ROWS)
        return carry

    lax.fori_loop(0, CX, step, 0)
    packed = jnp.concatenate([pack(total[...]), jnp.zeros((4, 128), F32)], axis=0)
    put_copies(out, packed)


def coarse_kernel(gathered, inverse, out, wide):
    for s in range(N_SUB):
        wide[32 * s : 32 * s + 32] = spread_rows(gathered[s, 0:4])
    rows = inverse[...].reshape(N_GRP * VEC, N_SUB * VEC)
    partial = dot3(split(rows), split(wide[...]), PLAIN)
    merge = (iota((128, 128), 0) % 16 == iota((128, 128), 1) % 16).astype(F32)
    partial = exact_dot(partial, merge)
    mine = iota(partial.shape, 0) % 8 == iota(partial.shape, 1) // 16
    partial = jnp.where(mine, partial, 0.0).reshape(N_GRP * 4, 8, 128).sum(axis=1)
    carried = add_up(gathered)[4:8]
    for g in range(N_GRP):
        out[g] = jnp.concatenate([partial[4 * g : 4 * g + 4], carried], axis=0)


def prolong_kernel(arrived, basis, field, scaling, keep, out, x_lo, x_hi, y_lo, y_hi, carried):
    total = add_up(arrived)
    carried[...] = total
    pick = iota((128, 128), 0) % 16 == iota((128, 128), 1) // 8
    values = exact_dot(spread_rows(total[0:4]), pick.astype(F32))
    matrix = split(kron_rows(values).T)

    def step(x, carry):
        product = dot3(matrix, split(slab(basis, x)), PLAIN)
        for h in range(2):
            cells = pl.ds(8 * h, 8)
            coarse = product[:, CZ * h : CZ * h + CZ].reshape(SRC, 8, CZ)
            out[:, x, cells, :] = scaling[x, cells, :] * field[:, x, cells, :] + coarse
        y_lo[:, pl.ds(x, 1), :] = keep[x, 0:1, :] * out[:, x, 0:1, :]
        y_hi[:, pl.ds(x, 1), :] = keep[x, 15:16, :] * out[:, x, 15:16, :]
        return carry

    lax.fori_loop(0, CX, step, 0)
    x_lo[...] = keep[0] * out[:, 0]
    x_hi[...] = keep[CX - 1] * out[:, CX - 1]


def stencil(x, j, field, x_lo, x_hi, y_lo, y_hi, coef, edge):
    rows = iota((CY, CZ), 0)
    v = field[j, x]
    if edge == 0:
        low, high = x_lo[j], field[j, x + 1]
    elif edge == 1:
        low, high = field[j, x - 1], x_hi[j]
    else:
        low, high = field[j, x - 1], field[j, x + 1]
    down = jnp.where(rows == 0, y_lo[j, pl.ds(x, 1), :], pltpu.roll(v, 1, 0))
    up = jnp.where(rows == CY - 1, y_hi[j, pl.ds(x, 1), :], pltpu.roll(v, CY - 1, 0))
    left, right = pltpu.roll(v, 1, 1), pltpu.roll(v, CZ - 1, 1)
    beside = coef[0, x] * low + coef[1, x] * high
    beside = beside + coef[2, x] * down + coef[3, x] * up
    beside = beside + coef[4, x] * left + coef[5, x] * right
    return coef[6, x] * v - beside


def apply_everywhere(field, x_lo, x_hi, y_lo, y_hi, coef, image):
    def plane(x, edge):
        for j in range(SRC):
            image[j, x] = stencil(x, j, field, x_lo, x_hi, y_lo, y_hi, coef, edge)

    def middle(x, carry):
        plane(x, 2)
        return carry

    plane(0, 0)
    lax.fori_loop(1, CX - 1, middle, 0)
    plane(CX - 1, 1)


def first_image_kernel(
    field, x_lo, x_hi, y_lo, y_hi, coef, basis, right_side, image, out, total, gram_a, gram_b
):
    apply_everywhere(field, x_lo, x_hi, y_lo, y_hi, coef, image)
    for ref in (total, gram_a, gram_b):
        ref[...] = jnp.zeros_like(ref)

    def step(x, carry):
        applied = split(slab(image, x))
        direction = split(slab(field, x))
        total[...] += dot3(split(slab(basis, x)), applied, ROWS_BY_ROWS)
        gram_a[...] += dot3(direction, split(slab(right_side, x)), ROWS_BY_ROWS)
        gram_b[...] += dot3(direction, applied, ROWS_BY_ROWS)
        return carry

    lax.fori_loop(0, CX, step, 0)
    packed = [pack(total[...]), pack(gram_a[...]), pack(gram_b[...])]
    put_copies(out, jnp.concatenate(packed, axis=0))


def second_image_kernel(
    field, x_lo, x_hi, y_lo, y_hi, coef, first_image, image, out, gram_c, gram_d
):
    apply_everywhere(field, x_lo, x_hi, y_lo, y_hi, coef, image)
    for ref in (gram_c, gram_d):
        ref[...] = jnp.zeros_like(ref)

    def step(x, carry):
        second = split(slab(field, x))
        gram_c[...] += dot3(split(slab(first_image, x)), second, ROWS_BY_ROWS)
        gram_d[...] += dot3(split(slab(image, x)), second, ROWS_BY_ROWS)
        return carry

    lax.fori_loop(0, CX, step, 0)
    cross = gram_c[...]
    packed = [pack(cross), pack(cross.T), pack(gram_d[...]), jnp.zeros((2, 128), F32)]
    put_copies(out, jnp.concatenate(packed, axis=0))


def relay_kernel(arrived, out):
    put_copies(out, add_up(arrived))


def eliminate(matrix):
    rows = iota(matrix.shape, 0)
    for p in range(16):
        row = matrix[p : p + 1] / matrix[p : p + 1, p : p + 1]
        column = matrix[:, p : p + 1]
        matrix = jnp.where(rows == p, row, matrix - column * row)
    return matrix


def tall(matrix):
    return jnp.concatenate([matrix, jnp.zeros((112, 128), F32)], axis=0)


def finish_kernel(
    arrived, carried, first, second, first_image, second_image, right_side, solution, residual
):
    total = add_up(arrived)
    cross, crossed, energy = total[0:2], total[2:4], total[4:6]
    projection, curvature = carried[4:6], carried[6:8]
    lanes = iota((16, 128), 1)
    solved = eliminate(unpack(curvature, 0) + unpack(projection, 16) + unpack(cross, 32))
    back = exact_dot(unpack(crossed, 0), tall(solved))
    reduced = unpack(energy, 0) - pltpu.roll(back, 96, 1)
    target = back - unpack(curvature, 16)
    last = eliminate(jnp.where(lanes < 16, reduced, jnp.where(lanes < 32, target, 0.0)))
    mix = jnp.where(lanes < 16, pltpu.roll(solved, 96, 1), 0.0)
    on_first = solved + exact_dot(mix, tall(last))
    pick = (iota((128, 128), 0) - 16 == iota((128, 128), 1) // 8).astype(F32)
    on_first = kron_rows(exact_dot(on_first, pick))
    on_second = kron_rows(exact_dot(-last, pick))
    matrix = split(jnp.concatenate([on_first, on_second], axis=0).T)

    def step(x, carry):
        pair = jnp.concatenate([slab(first, x), slab(second, x)], axis=0)
        images = jnp.concatenate([slab(first_image, x), slab(second_image, x)], axis=0)
        moved = dot3(matrix, split(pair), PLAIN)
        removed = dot3(matrix, split(images), PLAIN)
        for h in range(2):
            cells = pl.ds(8 * h, 8)
            part = slice(CZ * h, CZ * h + CZ)
            solution[:, x, cells, :] = moved[:, part].reshape(SRC, 8, CZ)
            residual[:, x, cells, :] = right_side[:, x, cells, :] - removed[:, part].reshape(
                SRC, 8, CZ
            )
        return carry

    lax.fori_loop(0, CX, step, 0)


INTERPRET = False


def call(kernel, out_shapes, scratch, *args):
    return pl.pallas_call(
        kernel,
        out_shape=[jax.ShapeDtypeStruct(s, F32) for s in out_shapes],
        in_specs=[pl.BlockSpec(memory_space=pltpu.VMEM)] * len(args),
        out_specs=[pl.BlockSpec(memory_space=pltpu.VMEM)] * len(out_shapes),
        scratch_shapes=[pltpu.VMEM(s, F32) for s in scratch],
        compiler_params=pltpu.CompilerParams(vmem_limit_bytes=48 * 1024 * 1024),
        interpret=INTERPRET,
    )(*args)


def exchange(pieces, axes):
    return lax.all_to_all(pieces, axes, split_axis=0, concat_axis=0, tiled=True)


def swap_edges(low, high, axes):
    count = lax.axis_size(axes)
    up = [(i, (i + 1) % count) for i in range(count)]
    return lax.ppermute(high, axes, up), lax.ppermute(low, axes, [(b, a) for a, b in up])


def local(right_side, conductivity, pinned_cells, coarse_basis, coarse_inverse):
    face = (SRC, CY, CZ)
    block = (CX, CY, CZ)
    tile = (8, 128)

    def coarse_answer(pieces):
        gathered = exchange(pieces, SUB)
        (partial,) = call(
            coarse_kernel, [(N_GRP, *tile)], [(N_SUB * VEC, 128)], gathered, coarse_inverse
        )
        return exchange(partial, GRP)

    def precondition(pieces, field):
        out = call(
            prolong_kernel,
            [FIELD, face, face, face, face, tile],
            [],
            coarse_answer(pieces),
            coarse_basis,
            field,
            scaling,
            keep,
        )
        smoothed, x_lo, x_hi, y_lo, y_hi, carried = out
        edges = (*swap_edges(x_lo, x_hi, GRP), *swap_edges(y_lo, y_hi, SUB))
        return smoothed, edges, carried

    x_edges = swap_edges(conductivity[0], conductivity[-1], GRP)
    y_edges = swap_edges(conductivity[:, 0], conductivity[:, -1], SUB)
    (pieces,) = call(
        restrict_kernel, [(N_SUB, *tile)], [(VEC * 8, 128)], coarse_basis, right_side
    )
    scaling, keep, coef = call(
        faces_kernel,
        [block, block, (7, *block)],
        [],
        conductivity,
        pinned_cells,
        *x_edges,
        *y_edges,
    )
    first, edges, _ = precondition(pieces, right_side)
    first_image, pieces = call(
        first_image_kernel,
        [FIELD, (N_SUB, *tile)],
        [(VEC * 8, 128), (128, 128), (128, 128)],
        first,
        *edges,
        coef,
        coarse_basis,
        right_side,
    )
    second, edges, carried = precondition(pieces, first_image)
    second_image, pieces = call(
        second_image_kernel,
        [FIELD, (N_GRP, *tile)],
        [(128, 128), (128, 128)],
        second,
        *edges,
        coef,
        first_image,
    )
    (pieces,) = call(relay_kernel, [(N_SUB, *tile)], [], exchange(pieces, GRP))
    return tuple(
        call(
            finish_kernel,
            [FIELD, FIELD],
            [],
            exchange(pieces, SUB),
            carried,
            first,
            second,
            first_image,
            second_image,
            right_side,
        )
    )


def solution(mesh):
    split_mesh = Mesh(
        mesh.devices.reshape(2, 4, 4, 4, 2), ("grp_0", "grp_1", "sub_0", "sub_1", "sub_2")
    )
    in_specs = (
        P(None, GRP, SUB, None),
        P(GRP, SUB, None),
        P(GRP, SUB, None),
        P(None, GRP, SUB, None),
        P(None, SUB, GRP),
    )
    out_specs = (P(None, GRP, SUB, None), P(None, GRP, SUB, None))
    return jax.shard_map(
        local, mesh=split_mesh, in_specs=in_specs, out_specs=out_specs, check_vma=False
    )
```

```python
import jax
import jax.numpy as jnp
from jax import lax
from jax.experimental import pallas as pl
from jax.experimental.pallas import tpu as pltpu
from jax.sharding import Mesh
from jax.sharding import PartitionSpec as P

GRP = ("grp_0", "grp_1")
SUB = ("sub_0", "sub_1", "sub_2")
N_GRP, N_SUB = 8, 32
F32, BF16 = jnp.float32, jnp.bfloat16
HIGHEST = lax.Precision.HIGHEST
CX, CY, CZ, SRC, VEC = 16, 16, 128, 16, 32
FIELD = (SRC, CX, CY, CZ)


def iota(shape, dim):
    return lax.broadcasted_iota(jnp.int32, shape, dim)


def exact_dot(left, right):
    return jnp.dot(left, right, precision=HIGHEST, preferred_element_type=F32)


def split(value):
    high = value.astype(BF16)
    return high, (value - high.astype(F32)).astype(BF16)


def dot3(left, right, by_rows):
    (lh, ll), (rh, rl) = left, right
    dim = 1 if by_rows else 0
    wide = jnp.concatenate([lh, lh, ll], axis=1)
    deep = jnp.concatenate([rh, rl, rh], axis=dim)
    return lax.dot_general(wide, deep, (((1,), (dim,)), ((), ())), preferred_element_type=F32)


def slab(ref, x):
    count = ref.shape[0]
    halves = [ref[:, x, 8 * h : 8 * h + 8, :].reshape(count * 8, CZ) for h in range(2)]
    return jnp.concatenate(halves, axis=1)


def rows_of(*pairs):
    return tuple(jnp.concatenate(parts, axis=0) for parts in zip(*pairs))


def pack(total):
    rows = total.shape[0]
    same = iota(total.shape, 0) % 8 == iota(total.shape, 1) % 8
    summed = jnp.where(same, total, 0.0).reshape(rows // 8, 8, 128).sum(axis=1)
    spread = exact_dot(summed, (iota((128, 128), 0) // 8 == iota((128, 128), 1) % 16).astype(F32))
    mine = iota(spread.shape, 0) % 8 == iota(spread.shape, 1) // 16
    return jnp.where(mine, spread, 0.0).reshape(rows // 64, 8, 128).sum(axis=1)


def spread_rows(packed):
    count = packed.shape[0]
    pieces = [jnp.broadcast_to(packed[r : r + 1], (8, 128)) for r in range(count)]
    wide = jnp.concatenate(pieces, axis=0)
    return jnp.where(iota(wide.shape, 0) % 8 == iota(wide.shape, 1) // 16, wide, 0.0)


def unpack(packed, offset):
    pick = iota((128, 128), 0) % 16 == iota((128, 128), 1) - offset
    return exact_dot(spread_rows(packed), pick.astype(F32))


def kron_rows(values):
    count = values.shape[0]
    pieces = [jnp.broadcast_to(values[n : n + 1], (8, 128)) for n in range(count)]
    wide = jnp.concatenate(pieces, axis=0)
    return jnp.where(iota(wide.shape, 0) % 8 == iota(wide.shape, 1) % 8, wide, 0.0)


def put_copies(out_ref, value):
    for n in range(out_ref.shape[0]):
        out_ref[n] = value


def add_up(ref):
    total = ref[0]
    for n in range(1, ref.shape[0]):
        total = total + ref[n]
    return total


def faces_kernel(cond, pinned, x_lo, x_hi, y_lo, y_hi, scaling, keep, coef, edge):
    g = lax.axis_index("grp_0") * 4 + lax.axis_index("grp_1")
    s = (lax.axis_index("sub_0") * 4 + lax.axis_index("sub_1")) * 2 + lax.axis_index("sub_2")

    def inside(count, flag):
        return jnp.broadcast_to(flag.astype(F32), (count, CZ))

    has_x_lo, has_x_hi = inside(CY, g > 0), inside(CY, g < N_GRP - 1)
    has_y_lo, has_y_hi = inside(1, s > 0), inside(1, s < N_SUB - 1)
    rows = iota((CY, CZ), 0)
    lanes = iota((CY, CZ), 1)

    def down(v, edge):
        return jnp.where(rows == 0, edge, pltpu.roll(v, 1, 0))

    def up(v, edge):
        return jnp.where(rows == CY - 1, edge, pltpu.roll(v, CY - 1, 0))

    def left(v):
        return jnp.where(lanes == 0, 0.0, pltpu.roll(v, 1, 1))

    def right(v):
        return jnp.where(lanes == CZ - 1, 0.0, pltpu.roll(v, CZ - 1, 1))

    for x in range(CX):
        keep[x] = 1.0 - pinned[x].astype(F32)
    for x in range(CX):
        c, k = cond[x], keep[x]
        c_lo = cond[x - 1] if x else has_x_lo * x_lo[...]
        c_hi = cond[x + 1] if x < CX - 1 else has_x_hi * x_hi[...]
        k_lo = keep[x - 1] if x else has_x_lo
        k_hi = keep[x + 1] if x < CX - 1 else has_x_hi
        beside = [
            (c_lo, k_lo),
            (c_hi, k_hi),
            (down(c, has_y_lo * y_lo[x : x + 1]), down(k, has_y_lo)),
            (up(c, has_y_hi * y_hi[x : x + 1]), up(k, has_y_hi)),
            (left(c), left(k)),
            (right(c), right(k)),
        ]
        centre = None
        for n, (other, mask) in enumerate(beside):
            face = 0.5 * (c + other)
            centre = face if centre is None else centre + face
            coef[n, x] = (k * mask) * face
        edge[0, x : x + 1] = coef[2, x, 0:1]
        edge[1, x : x + 1] = coef[3, x, CY - 1 : CY]
        coef[2, x, 0:1] = jnp.zeros((1, CZ), F32)
        coef[3, x, CY - 1 : CY] = jnp.zeros((1, CZ), F32)
        whole = k * centre + (1.0 - k)
        coef[6, x] = whole
        scaling[x] = 1.0 / whole


CHUNKS = 4
DEEP = CX // CHUNKS


def chunk_copies(pairs, sems):
    return [
        [
            pltpu.make_async_copy(
                src.at[:, pl.ds(c * DEEP, DEEP)], dst.at[:, pl.ds(c * DEEP, DEEP)], sems.at[c, n]
            )
            for n, (src, dst) in enumerate(pairs)
        ]
        for c in range(CHUNKS)
    ]


def start_all(copies):
    for chunk in copies:
        for copy in chunk:
            copy.start()


def wait_all(chunk):
    for copy in chunk:
        copy.wait()


def restrict_kernel(basis_hbm, field_hbm, out, basis, field, total, sems):
    copies = chunk_copies(((basis_hbm, basis), (field_hbm, field)), sems)
    start_all(copies)
    total[...] = jnp.zeros_like(total)
    for c in range(CHUNKS):
        wait_all(copies[c])
        for x in range(c * DEEP, (c + 1) * DEEP):
            total[...] += dot3(split(slab(basis, x)), split(slab(field, x)), True)
    packed = jnp.concatenate([pack(total[...]), jnp.zeros((4, 128), F32)], axis=0)
    put_copies(out, packed)


def coarse_kernel(gathered, inverse, out, wide):
    for s in range(N_SUB):
        wide[32 * s : 32 * s + 32] = spread_rows(gathered[s, 0:4])
    rows = inverse[...].reshape(N_GRP * VEC, N_SUB * VEC)
    partial = dot3(split(rows), split(wide[...]), False)
    merge = (iota((128, 128), 0) % 16 == iota((128, 128), 1) % 16).astype(F32)
    partial = exact_dot(partial, merge)
    mine = iota(partial.shape, 0) % 8 == iota(partial.shape, 1) // 16
    partial = jnp.where(mine, partial, 0.0).reshape(N_GRP * 4, 8, 128).sum(axis=1)
    carried = add_up(gathered)[4:8]
    for g in range(N_GRP):
        out[g] = jnp.concatenate([partial[4 * g : 4 * g + 4], carried], axis=0)


def prolong_kernel(
    arrived, basis_hbm, field_hbm, scaling, keep, out, x_lo, x_hi, y_lo, y_hi, carried,
    basis, field, sems,
):
    copies = chunk_copies(((basis_hbm, basis), (field_hbm, field)), sems)
    start_all(copies)
    total = add_up(arrived)
    carried[...] = total
    pick = iota((128, 128), 0) % 16 == iota((128, 128), 1) // 8
    values = exact_dot(spread_rows(total[0:4]), pick.astype(F32))
    matrix = split(kron_rows(values).T)
    for c in range(CHUNKS):
        wait_all(copies[c])
        for x in range(c * DEEP, (c + 1) * DEEP):
            product = dot3(matrix, split(slab(basis, x)), False)
            halves = []
            for h in range(2):
                cells = slice(8 * h, 8 * h + 8)
                coarse = product[:, CZ * h : CZ * h + CZ].reshape(SRC, 8, CZ)
                halves.append(scaling[x, cells, :] * field[:, x, cells, :] + coarse)
                out[:, x, cells, :] = halves[h]
            y_lo[:, x : x + 1, :] = keep[x, 0:1, :] * halves[0][:, 0:1, :]
            y_hi[:, x : x + 1, :] = keep[x, 15:16, :] * halves[1][:, 7:8, :]
            for edge, face in ((0, x_lo), (CX - 1, x_hi)):
                if x == edge:
                    face[:, 0:8, :] = keep[x, 0:8, :] * halves[0]
                    face[:, 8:16, :] = keep[x, 8:16, :] * halves[1]


def inner_kernel(field, coef, image):
    def plane(x, low, high):
        for j in range(SRC):
            v = field[j, x]
            beside = coef[2, x] * pltpu.roll(v, 1, 0) + coef[3, x] * pltpu.roll(v, CY - 1, 0)
            beside = beside + coef[4, x] * pltpu.roll(v, 1, 1)
            beside = beside + coef[5, x] * pltpu.roll(v, CZ - 1, 1)
            if low:
                beside = beside + coef[0, x] * field[j, x - 1]
            if high:
                beside = beside + coef[1, x] * field[j, x + 1]
            image[j, x] = coef[6, x] * v - beside

    def middle(i, carry):
        plane(2 * i + 1, True, True)
        plane(2 * i + 2, True, True)
        return carry

    plane(0, False, True)
    lax.fori_loop(0, CX // 2 - 1, middle, 0)
    plane(CX - 1, True, False)


def whole_plane(x, inner, y_lo, y_hi, edge):
    rows = iota((8, CZ), 0)
    low = jnp.where(rows == 0, edge[0, pl.ds(x, 1), :] * y_lo[:, pl.ds(x, 1), :], 0.0)
    high = jnp.where(rows == 7, edge[1, pl.ds(x, 1), :] * y_hi[:, pl.ds(x, 1), :], 0.0)
    return inner[:, x, 0:8, :] - low, inner[:, x, 8:16, :] - high


def side_by_side(halves):
    return jnp.concatenate([h.reshape(SRC * 8, CZ) for h in halves], axis=1)


def by_chunks(plane, inner, image, arriving, copies):
    for c in range(CHUNKS):
        wait_all(arriving[c])
        for x in range(c * DEEP, (c + 1) * DEEP):
            plane(x, image if x in (0, CX - 1) else inner)
        for copy in copies[c]:
            copy.start()
    for c in range(CHUNKS):
        wait_all(copies[c])


def first_image_kernel(
    inner, x_lo, x_hi, y_lo, y_hi, coef, edge, field, basis_hbm, right_side_hbm, image_hbm, out,
    image, total, gram, basis, right_side, sems, in_sems,
):
    arriving = chunk_copies(((basis_hbm, basis), (right_side_hbm, right_side)), in_sems)
    start_all(arriving)
    image[:, 0] = inner[:, 0] - coef[0, 0] * x_lo[...]
    image[:, CX - 1] = inner[:, CX - 1] - coef[1, CX - 1] * x_hi[...]
    total[...] = jnp.zeros_like(total)
    gram[...] = jnp.zeros_like(gram)

    def plane(x, source):
        halves = whole_plane(x, source, y_lo, y_hi, edge)
        image[:, x, 0:8, :], image[:, x, 8:16, :] = halves
        applied = split(side_by_side(halves))
        direction = split(slab(field, x))
        total[...] += dot3(rows_of(split(slab(basis, x)), direction), applied, True)
        gram[...] += dot3(direction, split(slab(right_side, x)), True)

    by_chunks(plane, inner, image, arriving, chunk_copies(((image, image_hbm),), sems))
    packed = [pack(total[0 : VEC * 8]), pack(gram[...]), pack(total[VEC * 8 :])]
    put_copies(out, jnp.concatenate(packed, axis=0))


def second_image_kernel(
    inner, x_lo, x_hi, y_lo, y_hi, coef, edge, field, first_image_hbm, image_hbm, out,
    image, total, first_image, sems, in_sems,
):
    arriving = chunk_copies(((first_image_hbm, first_image),), in_sems)
    start_all(arriving)
    image[:, 0] = inner[:, 0] - coef[0, 0] * x_lo[...]
    image[:, CX - 1] = inner[:, CX - 1] - coef[1, CX - 1] * x_hi[...]
    total[...] = jnp.zeros_like(total)

    def plane(x, source):
        halves = whole_plane(x, source, y_lo, y_hi, edge)
        image[:, x, 0:8, :], image[:, x, 8:16, :] = halves
        pair = rows_of(split(slab(first_image, x)), split(side_by_side(halves)))
        total[...] += dot3(pair, split(slab(field, x)), True)

    by_chunks(plane, inner, image, arriving, chunk_copies(((image, image_hbm),), sems))
    cross = total[0:128]
    packed = [pack(cross), pack(cross.T), pack(total[128:256]), jnp.zeros((2, 128), F32)]
    put_copies(out, jnp.concatenate(packed, axis=0))


def relay_kernel(arrived, out):
    put_copies(out, add_up(arrived))


def eliminate(matrix):
    rows = iota(matrix.shape, 0)
    for p in range(16):
        row = matrix[p : p + 1] / matrix[p : p + 1, p : p + 1]
        column = matrix[:, p : p + 1]
        matrix = jnp.where(rows == p, row, matrix - column * row)
    return matrix


def tall(matrix):
    return jnp.concatenate([matrix, jnp.zeros((112, 128), F32)], axis=0)


def early_kernel(carried, out):
    projection, curvature = carried[4:6], carried[6:8]
    unit = (iota((16, 128), 0) == iota((16, 128), 1) - 32).astype(F32)
    out[...] = eliminate(unpack(curvature, 0) + unpack(projection, 16) + unit)


def finish_kernel(
    arrived, carried, early, first_hbm, second_hbm, first_image_hbm, second_image_hbm,
    right_side_hbm, solution_hbm, residual_hbm,
    first, second, first_image, second_image, right_side, solution, residual, sems, out_sems,
):
    copies = chunk_copies(
        (
            (first_hbm, first),
            (second_hbm, second),
            (first_image_hbm, first_image),
            (second_image_hbm, second_image),
            (right_side_hbm, right_side),
        ),
        sems,
    )
    start_all(copies)
    total = add_up(arrived)
    cross, crossed, energy = total[0:2], total[2:4], total[4:6]
    curvature = carried[6:8]
    lanes = iota((16, 128), 1)
    early_part = early[...]
    inverse = jnp.where(lanes < 16, pltpu.roll(early_part, 96, 1), 0.0)
    mixed = exact_dot(inverse, tall(unpack(cross, 32)))
    solved = jnp.where(lanes < 32, early_part, mixed)
    back = exact_dot(unpack(crossed, 0), tall(solved))
    reduced = unpack(energy, 0) - pltpu.roll(back, 96, 1)
    target = back - unpack(curvature, 16)
    last = eliminate(jnp.where(lanes < 16, reduced, jnp.where(lanes < 32, target, 0.0)))
    mix = jnp.where(lanes < 16, pltpu.roll(mixed, 96, 1), 0.0)
    on_first = early_part + exact_dot(mix, tall(last))
    pick = (iota((128, 128), 0) - 16 == iota((128, 128), 1) // 8).astype(F32)
    on_first = kron_rows(exact_dot(on_first, pick))
    on_second = kron_rows(exact_dot(-last, pick))
    matrix = split(jnp.concatenate([on_first, on_second], axis=0).T)

    out_copies = chunk_copies(((solution, solution_hbm), (residual, residual_hbm)), out_sems)
    for c in range(CHUNKS):
        wait_all(copies[c])
        for x in range(c * DEEP, (c + 1) * DEEP):
            pair = rows_of(split(slab(first, x)), split(slab(second, x)))
            images = rows_of(split(slab(first_image, x)), split(slab(second_image, x)))
            moved, removed = dot3(matrix, pair, False), dot3(matrix, images, False)
            for h in range(2):
                cells = slice(8 * h, 8 * h + 8)
                part = slice(CZ * h, CZ * h + CZ)
                solution[:, x, cells, :] = moved[:, part].reshape(SRC, 8, CZ)
                left_over = right_side[:, x, cells, :] - removed[:, part].reshape(SRC, 8, CZ)
                residual[:, x, cells, :] = left_over
        for copy in out_copies[c]:
            copy.start()
    for c in range(CHUNKS):
        wait_all(out_copies[c])


VMEM, HBM = pltpu.VMEM, pltpu.HBM
MIB = 1024 * 1024
FULL_LIMIT, PROLONG_LIMIT, IMAGE_LIMIT = 58, 50, 46


def call(kernel, outs, scratch, *args, far=(), limit=16):
    specs = [
        pl.BlockSpec(memory_space=HBM if n in far else VMEM) for n in range(len(args) + len(outs))
    ]
    return pl.pallas_call(
        kernel,
        out_shape=[jax.ShapeDtypeStruct(shape, F32) for shape in outs],
        in_specs=specs[: len(args)],
        out_specs=specs[len(args) :],
        scratch_shapes=[pltpu.VMEM(s, F32) if isinstance(s, tuple) else s for s in scratch],
        compiler_params=pltpu.CompilerParams(vmem_limit_bytes=limit * MIB),
    )(*args)


def exchange(pieces, axes):
    return lax.all_to_all(pieces, axes, split_axis=0, concat_axis=0, tiled=True)


def swap_edges(low, high, axes):
    count = lax.axis_size(axes)
    up = [(i, (i + 1) % count) for i in range(count)]
    return lax.ppermute(high, axes, up), lax.ppermute(low, axes, [(b, a) for a, b in up])


def copy_sems(count):
    return pltpu.SemaphoreType.DMA((CHUNKS, count))


def local(right_side, conductivity, pinned_cells, coarse_basis, coarse_inverse):
    face = (SRC, CY, CZ)
    block = (CX, CY, CZ)
    tile = (8, 128)
    bases = (VEC, *block)

    def coarse_answer(pieces):
        gathered = exchange(pieces, SUB)
        (partial,) = call(
            coarse_kernel, [(N_GRP, *tile)], [(N_SUB * VEC, 128)], gathered, coarse_inverse
        )
        return exchange(partial, GRP)

    def precondition(pieces, field):
        smoothed, x_lo, x_hi, y_lo, y_hi, carried = call(
            prolong_kernel,
            [FIELD, face, face, face, face, tile],
            [bases, FIELD, copy_sems(2)],
            coarse_answer(pieces),
            coarse_basis,
            field,
            scaling,
            keep,
            far=(1, 2),
            limit=PROLONG_LIMIT,
        )
        edges = (*swap_edges(x_lo, x_hi, GRP), *swap_edges(y_lo, y_hi, SUB))
        (inner,) = call(inner_kernel, [FIELD], [], smoothed, coef)
        return smoothed, (inner, *edges, coef, edge), carried

    x_edges = swap_edges(conductivity[0], conductivity[-1], GRP)
    y_edges = swap_edges(conductivity[:, 0], conductivity[:, -1], SUB)
    (pieces,) = call(
        restrict_kernel,
        [(N_SUB, *tile)],
        [bases, FIELD, (VEC * 8, 128), copy_sems(2)],
        coarse_basis,
        right_side,
        far=(0, 1),
        limit=FULL_LIMIT,
    )
    scaling, keep, coef, edge = call(
        faces_kernel,
        [block, block, (7, *block), (2, CX, CZ)],
        [],
        conductivity,
        pinned_cells,
        *x_edges,
        *y_edges,
    )
    first, inner, _ = precondition(pieces, right_side)
    first_image, pieces = call(
        first_image_kernel,
        [FIELD, (N_SUB, *tile)],
        [FIELD, (VEC * 8 + 128, 128), (128, 128), bases, FIELD, copy_sems(1), copy_sems(2)],
        *inner,
        first,
        coarse_basis,
        right_side,
        far=(8, 9, 10),
        limit=IMAGE_LIMIT,
    )
    second, inner, carried = precondition(pieces, first_image)
    (early,) = call(early_kernel, [(16, 128)], [], carried)
    second_image, pieces = call(
        second_image_kernel,
        [FIELD, (N_GRP, *tile)],
        [FIELD, (256, 128), FIELD, copy_sems(1), copy_sems(1)],
        *inner,
        second,
        first_image,
        far=(8, 9),
        limit=IMAGE_LIMIT,
    )
    (pieces,) = call(relay_kernel, [(N_SUB, *tile)], [], exchange(pieces, GRP))
    return tuple(
        call(
            finish_kernel,
            [FIELD, FIELD],
            [FIELD] * 7 + [copy_sems(5), copy_sems(2)],
            exchange(pieces, SUB),
            carried,
            early,
            first,
            second,
            first_image,
            second_image,
            right_side,
            far=(3, 4, 5, 6, 7, 8, 9),
            limit=FULL_LIMIT,
        )
    )


def solution(mesh):
    split_mesh = Mesh(
        mesh.devices.reshape(2, 4, 4, 4, 2), ("grp_0", "grp_1", "sub_0", "sub_1", "sub_2")
    )
    in_specs = (
        P(None, GRP, SUB, None),
        P(GRP, SUB, None),
        P(GRP, SUB, None),
        P(None, GRP, SUB, None),
        P(None, SUB, GRP),
    )
    out_specs = (P(None, GRP, SUB, None), P(None, GRP, SUB, None))
    return jax.shard_map(
        local, mesh=split_mesh, in_specs=in_specs, out_specs=out_specs, check_vma=False
    )
```

```python
import jax
import jax.numpy as jnp
from jax import lax
from jax.experimental import pallas as pl
from jax.experimental.pallas import tpu as pltpu
from jax.sharding import Mesh
from jax.sharding import PartitionSpec as P

GRP = ("grp_0", "grp_1")
SUB = ("sub_0", "sub_1", "sub_2")
N_GRP, N_SUB = 8, 32
F32, BF16 = jnp.float32, jnp.bfloat16
HIGHEST = lax.Precision.HIGHEST
CX, CY, CZ, SRC, VEC = 16, 16, 128, 16, 32
FIELD = (SRC, CX, CY, CZ)


def iota(shape, dim):
    return lax.broadcasted_iota(jnp.int32, shape, dim)


def exact_dot(left, right):
    return jnp.dot(left, right, precision=HIGHEST, preferred_element_type=F32)


def split(value):
    high = value.astype(BF16)
    return high, (value - high.astype(F32)).astype(BF16)


def dot3(left, right, by_rows):
    (lh, ll), (rh, rl) = left, right
    dim = 1 if by_rows else 0
    wide = jnp.concatenate([lh, lh, ll], axis=1)
    deep = jnp.concatenate([rh, rl, rh], axis=dim)
    return lax.dot_general(wide, deep, (((1,), (dim,)), ((), ())), preferred_element_type=F32)


def slab(ref, x):
    count = ref.shape[0]
    halves = [ref[:, x, 8 * h : 8 * h + 8, :].reshape(count * 8, CZ) for h in range(2)]
    return jnp.concatenate(halves, axis=1)


def rows_of(*pairs):
    return tuple(jnp.concatenate(parts, axis=0) for parts in zip(*pairs))


def pack(total):
    rows = total.shape[0]
    same = iota(total.shape, 0) % 8 == iota(total.shape, 1) % 8
    summed = jnp.where(same, total, 0.0).reshape(rows // 8, 8, 128).sum(axis=1)
    spread = exact_dot(summed, (iota((128, 128), 0) // 8 == iota((128, 128), 1) % 16).astype(F32))
    mine = iota(spread.shape, 0) % 8 == iota(spread.shape, 1) // 16
    return jnp.where(mine, spread, 0.0).reshape(rows // 64, 8, 128).sum(axis=1)


def spread_rows(packed):
    count = packed.shape[0]
    pieces = [jnp.broadcast_to(packed[r : r + 1], (8, 128)) for r in range(count)]
    wide = jnp.concatenate(pieces, axis=0)
    return jnp.where(iota(wide.shape, 0) % 8 == iota(wide.shape, 1) // 16, wide, 0.0)


def unpack(packed, offset):
    pick = iota((128, 128), 0) % 16 == iota((128, 128), 1) - offset
    return exact_dot(spread_rows(packed), pick.astype(F32))


def kron_rows(values):
    count = values.shape[0]
    pieces = [jnp.broadcast_to(values[n : n + 1], (8, 128)) for n in range(count)]
    wide = jnp.concatenate(pieces, axis=0)
    return jnp.where(iota(wide.shape, 0) % 8 == iota(wide.shape, 1) % 8, wide, 0.0)


def put_copies(out_ref, value):
    for n in range(out_ref.shape[0]):
        out_ref[n] = value


def add_up(ref):
    total = ref[0]
    for n in range(1, ref.shape[0]):
        total = total + ref[n]
    return total


def position():
    g = lax.axis_index("grp_0") * 4 + lax.axis_index("grp_1")
    return g, (lax.axis_index("sub_0") * 4 + lax.axis_index("sub_1")) * 2 + lax.axis_index("sub_2")


def in_order(place, first, second):
    even = place % 2 == 0
    return jnp.where(even, first, second), jnp.where(even, second, first)


def faces_kernel(cond, pinned, x_a, x_b, y_a, y_b, scaling, keep, coef, edge):
    g, s = position()

    def inside(count, flag):
        return jnp.broadcast_to(flag.astype(F32), (count, CZ))

    x_hi, x_lo = in_order(g, x_a[...], x_b[...])
    y_hi, y_lo = in_order(s, y_a[...], y_b[...])
    has_x_lo, has_x_hi = inside(CY, g > 0), inside(CY, g < N_GRP - 1)
    has_y_lo, has_y_hi = inside(1, s > 0), inside(1, s < N_SUB - 1)
    rows = iota((CY, CZ), 0)
    lanes = iota((CY, CZ), 1)

    def down(v, edge):
        return jnp.where(rows == 0, edge, pltpu.roll(v, 1, 0))

    def up(v, edge):
        return jnp.where(rows == CY - 1, edge, pltpu.roll(v, CY - 1, 0))

    def left(v):
        return jnp.where(lanes == 0, 0.0, pltpu.roll(v, 1, 1))

    def right(v):
        return jnp.where(lanes == CZ - 1, 0.0, pltpu.roll(v, CZ - 1, 1))

    for x in range(CX):
        keep[x] = 1.0 - pinned[x].astype(F32)
    for x in range(CX):
        c, k = cond[x], keep[x]
        c_lo = cond[x - 1] if x else has_x_lo * x_lo
        c_hi = cond[x + 1] if x < CX - 1 else has_x_hi * x_hi
        k_lo = keep[x - 1] if x else has_x_lo
        k_hi = keep[x + 1] if x < CX - 1 else has_x_hi
        beside = [
            (c_lo, k_lo),
            (c_hi, k_hi),
            (down(c, has_y_lo * y_lo[x : x + 1]), down(k, has_y_lo)),
            (up(c, has_y_hi * y_hi[x : x + 1]), up(k, has_y_hi)),
            (left(c), left(k)),
            (right(c), right(k)),
        ]
        centre = None
        for n, (other, mask) in enumerate(beside):
            face = 0.5 * (c + other)
            centre = face if centre is None else centre + face
            coef[n, x] = (k * mask) * face
        edge[0, x : x + 1] = coef[2, x, 0:1]
        edge[1, x : x + 1] = coef[3, x, CY - 1 : CY]
        coef[2, x, 0:1] = jnp.zeros((1, CZ), F32)
        coef[3, x, CY - 1 : CY] = jnp.zeros((1, CZ), F32)
        whole = k * centre + (1.0 - k)
        coef[6, x] = whole
        scaling[x] = 1.0 / whole


CHUNKS = 4
DEEP = CX // CHUNKS


def chunk_copies(pairs, sems):
    return [
        [
            pltpu.make_async_copy(
                src.at[:, pl.ds(c * DEEP, DEEP)], dst.at[:, pl.ds(c * DEEP, DEEP)], sems.at[c, n]
            )
            for n, (src, dst) in enumerate(pairs)
        ]
        for c in range(CHUNKS)
    ]


def start_all(copies):
    for chunk in copies:
        for copy in chunk:
            copy.start()


def wait_all(chunk):
    for copy in chunk:
        copy.wait()


def restrict_kernel(basis_hbm, field_hbm, out, basis, field, total, sems):
    copies = chunk_copies(((basis_hbm, basis), (field_hbm, field)), sems)
    start_all(copies)
    total[...] = jnp.zeros_like(total)
    for c in range(CHUNKS):
        wait_all(copies[c])
        for x in range(c * DEEP, (c + 1) * DEEP):
            total[...] += dot3(split(slab(basis, x)), split(slab(field, x)), True)
    packed = jnp.concatenate([pack(total[...]), jnp.zeros((4, 128), F32)], axis=0)
    put_copies(out, packed)


def coarse_kernel(gathered, inverse, out, wide):
    for s in range(N_SUB):
        wide[32 * s : 32 * s + 32] = spread_rows(gathered[s, 0:4])
    rows = inverse[...].reshape(N_GRP * VEC, N_SUB * VEC)
    partial = dot3(split(rows), split(wide[...]), False)
    merge = (iota((128, 128), 0) % 16 == iota((128, 128), 1) % 16).astype(F32)
    partial = exact_dot(partial, merge)
    mine = iota(partial.shape, 0) % 8 == iota(partial.shape, 1) // 16
    partial = jnp.where(mine, partial, 0.0).reshape(N_GRP * 4, 8, 128).sum(axis=1)
    carried = add_up(gathered)[4:8]
    for g in range(N_GRP):
        out[g] = jnp.concatenate([partial[4 * g : 4 * g + 4], carried], axis=0)


def prolong_kernel(
    arrived, basis_hbm, field_hbm, scaling, keep, out, x_a, x_b, y_a, y_b, carried,
    basis, field, sems,
):
    copies = chunk_copies(((basis_hbm, basis), (field_hbm, field)), sems)
    start_all(copies)
    g, s = position()
    total = add_up(arrived)
    carried[...] = total
    pick = iota((128, 128), 0) % 16 == iota((128, 128), 1) // 8
    values = exact_dot(spread_rows(total[0:4]), pick.astype(F32))
    matrix = split(kron_rows(values).T)
    for c in range(CHUNKS):
        wait_all(copies[c])
        for x in range(c * DEEP, (c + 1) * DEEP):
            product = dot3(matrix, split(slab(basis, x)), False)
            halves = []
            for h in range(2):
                cells = slice(8 * h, 8 * h + 8)
                coarse = product[:, CZ * h : CZ * h + CZ].reshape(SRC, 8, CZ)
                halves.append(scaling[x, cells, :] * field[:, x, cells, :] + coarse)
                out[:, x, cells, :] = halves[h]
            ends = (keep[x, 0:1, :] * halves[0][:, 0:1, :], keep[x, 15:16, :] * halves[1][:, 7:8, :])
            y_a[:, x : x + 1, :], y_b[:, x : x + 1, :] = in_order(s, ends[1], ends[0])
    low, high = keep[0] * out[:, 0], keep[CX - 1] * out[:, CX - 1]
    x_a[...], x_b[...] = in_order(g, high, low)


def inner_kernel(field, coef, image):
    inner_planes(field, coef, image)


def inner_and_early_kernel(field, coef, carried, image, early):
    projection, curvature = carried[4:6], carried[6:8]
    unit = (iota((16, 128), 0) == iota((16, 128), 1) - 32).astype(F32)
    early[...] = eliminate(unpack(curvature, 0) + unpack(projection, 16) + unit)
    inner_planes(field, coef, image)


def inner_planes(field, coef, image):
    def plane(x, low, high):
        for j in range(SRC):
            v = field[j, x]
            beside = coef[2, x] * pltpu.roll(v, 1, 0) + coef[3, x] * pltpu.roll(v, CY - 1, 0)
            beside = beside + coef[4, x] * pltpu.roll(v, 1, 1)
            beside = beside + coef[5, x] * pltpu.roll(v, CZ - 1, 1)
            if low:
                beside = beside + coef[0, x] * field[j, x - 1]
            if high:
                beside = beside + coef[1, x] * field[j, x + 1]
            image[j, x] = coef[6, x] * v - beside

    def middle(i, carry):
        plane(2 * i + 1, True, True)
        plane(2 * i + 2, True, True)
        return carry

    plane(0, False, True)
    lax.fori_loop(0, CX // 2 - 1, middle, 0)
    plane(CX - 1, True, False)


def whole_plane(x, s, inner, y_a, y_b, edge):
    rows = iota((8, CZ), 0)
    y_hi, y_lo = in_order(s, y_a[:, x : x + 1, :], y_b[:, x : x + 1, :])
    low = jnp.where(rows == 0, edge[0, x : x + 1, :] * y_lo, 0.0)
    high = jnp.where(rows == 7, edge[1, x : x + 1, :] * y_hi, 0.0)
    return inner[:, x, 0:8, :] - low, inner[:, x, 8:16, :] - high


def side_by_side(halves):
    return jnp.concatenate([h.reshape(SRC * 8, CZ) for h in halves], axis=1)


def by_chunks(plane, inner, image, arriving, copies):
    for c in range(CHUNKS):
        wait_all(arriving[c])
        for x in range(c * DEEP, (c + 1) * DEEP):
            plane(x, image if x in (0, CX - 1) else inner)
        for copy in copies[c]:
            copy.start()
    for c in range(CHUNKS):
        wait_all(copies[c])


def first_image_kernel(
    inner, x_a, x_b, y_a, y_b, coef, edge, field, basis_hbm, right_side_hbm, image_hbm, out,
    image, total, gram, basis, right_side, sems, in_sems,
):
    arriving = chunk_copies(((basis_hbm, basis), (right_side_hbm, right_side)), in_sems)
    start_all(arriving)
    g, s = position()
    x_hi, x_lo = in_order(g, x_a[...], x_b[...])
    image[:, 0] = inner[:, 0] - coef[0, 0] * x_lo
    image[:, CX - 1] = inner[:, CX - 1] - coef[1, CX - 1] * x_hi
    total[...] = jnp.zeros_like(total)
    gram[...] = jnp.zeros_like(gram)

    def plane(x, source):
        halves = whole_plane(x, s, source, y_a, y_b, edge)
        image[:, x, 0:8, :], image[:, x, 8:16, :] = halves
        applied = split(side_by_side(halves))
        direction = split(slab(field, x))
        total[...] += dot3(rows_of(split(slab(basis, x)), direction), applied, True)
        gram[...] += dot3(direction, split(slab(right_side, x)), True)

    by_chunks(plane, inner, image, arriving, chunk_copies(((image, image_hbm),), sems))
    packed = [pack(total[0 : VEC * 8]), pack(gram[...]), pack(total[VEC * 8 :])]
    put_copies(out, jnp.concatenate(packed, axis=0))


def second_image_kernel(
    inner, x_a, x_b, y_a, y_b, coef, edge, field, first_image_hbm, image_hbm, out,
    image, total, first_image, sems, in_sems,
):
    arriving = chunk_copies(((first_image_hbm, first_image),), in_sems)
    start_all(arriving)
    g, s = position()
    x_hi, x_lo = in_order(g, x_a[...], x_b[...])
    image[:, 0] = inner[:, 0] - coef[0, 0] * x_lo
    image[:, CX - 1] = inner[:, CX - 1] - coef[1, CX - 1] * x_hi
    total[...] = jnp.zeros_like(total)

    def plane(x, source):
        halves = whole_plane(x, s, source, y_a, y_b, edge)
        image[:, x, 0:8, :], image[:, x, 8:16, :] = halves
        pair = rows_of(split(slab(first_image, x)), split(side_by_side(halves)))
        total[...] += dot3(pair, split(slab(field, x)), True)

    by_chunks(plane, inner, image, arriving, chunk_copies(((image, image_hbm),), sems))
    cross = total[0:128]
    packed = [pack(cross), pack(cross.T), pack(total[128:256]), jnp.zeros((2, 128), F32)]
    put_copies(out, jnp.concatenate(packed, axis=0))


def relay_kernel(arrived, out):
    put_copies(out, add_up(arrived))


def eliminate(matrix):
    rows = iota(matrix.shape, 0)
    for p in range(16):
        row = matrix[p : p + 1] / matrix[p : p + 1, p : p + 1]
        column = matrix[:, p : p + 1]
        matrix = jnp.where(rows == p, row, matrix - column * row)
    return matrix


def tall(matrix):
    return jnp.concatenate([matrix, jnp.zeros((112, 128), F32)], axis=0)


def finish_kernel(
    arrived, carried, early, first_hbm, second_hbm, first_image_hbm, second_image_hbm,
    right_side_hbm, solution_hbm, residual_hbm,
    first, second, first_image, second_image, right_side, solution, residual, sems, out_sems,
):
    copies = chunk_copies(
        (
            (first_hbm, first),
            (second_hbm, second),
            (first_image_hbm, first_image),
            (second_image_hbm, second_image),
            (right_side_hbm, right_side),
        ),
        sems,
    )
    start_all(copies)
    total = add_up(arrived)
    cross, crossed, energy = total[0:2], total[2:4], total[4:6]
    curvature = carried[6:8]
    lanes = iota((16, 128), 1)
    early_part = early[...]
    inverse = jnp.where(lanes < 16, pltpu.roll(early_part, 96, 1), 0.0)
    mixed = exact_dot(inverse, tall(unpack(cross, 32)))
    solved = jnp.where(lanes < 32, early_part, mixed)
    back = exact_dot(unpack(crossed, 0), tall(solved))
    reduced = unpack(energy, 0) - pltpu.roll(back, 96, 1)
    target = back - unpack(curvature, 16)
    last = eliminate(jnp.where(lanes < 16, reduced, jnp.where(lanes < 32, target, 0.0)))
    mix = jnp.where(lanes < 16, pltpu.roll(mixed, 96, 1), 0.0)
    on_first = early_part + exact_dot(mix, tall(last))
    pick = (iota((128, 128), 0) - 16 == iota((128, 128), 1) // 8).astype(F32)
    on_first = kron_rows(exact_dot(on_first, pick))
    on_second = kron_rows(exact_dot(-last, pick))
    matrix = split(jnp.concatenate([on_first, on_second], axis=0).T)

    out_copies = chunk_copies(((solution, solution_hbm), (residual, residual_hbm)), out_sems)
    for c in range(CHUNKS):
        wait_all(copies[c])
        for x in range(c * DEEP, (c + 1) * DEEP):
            pair = rows_of(split(slab(first, x)), split(slab(second, x)))
            images = rows_of(split(slab(first_image, x)), split(slab(second_image, x)))
            moved, removed = dot3(matrix, pair, False), dot3(matrix, images, False)
            for h in range(2):
                cells = slice(8 * h, 8 * h + 8)
                part = slice(CZ * h, CZ * h + CZ)
                solution[:, x, cells, :] = moved[:, part].reshape(SRC, 8, CZ)
                left_over = right_side[:, x, cells, :] - removed[:, part].reshape(SRC, 8, CZ)
                residual[:, x, cells, :] = left_over
        for copy in out_copies[c]:
            copy.start()
    for c in range(CHUNKS):
        wait_all(out_copies[c])


VMEM, HBM = pltpu.VMEM, pltpu.HBM
MIB = 1024 * 1024
FULL_LIMIT, PROLONG_LIMIT, IMAGE_LIMIT = 58, 50, 46


def call(kernel, outs, scratch, *args, far=(), limit=16):
    specs = [
        pl.BlockSpec(memory_space=HBM if n in far else VMEM) for n in range(len(args) + len(outs))
    ]
    return pl.pallas_call(
        kernel,
        out_shape=[jax.ShapeDtypeStruct(shape, F32) for shape in outs],
        in_specs=specs[: len(args)],
        out_specs=specs[len(args) :],
        scratch_shapes=[pltpu.VMEM(s, F32) if isinstance(s, tuple) else s for s in scratch],
        compiler_params=pltpu.CompilerParams(vmem_limit_bytes=limit * MIB),
    )(*args)


def exchange(pieces, axes):
    return lax.all_to_all(pieces, axes, split_axis=0, concat_axis=0, tiled=True)


def swap_edges(x_a, x_b, y_a, y_b):
    def swap(array, axes, first):
        count = lax.axis_size(axes)
        partner = [i + 1 if i % 2 == first else i - 1 for i in range(count)]
        pairs = [(i, p if 0 <= p < count else i) for i, p in enumerate(partner)]
        return lax.ppermute(array, axes, pairs)

    y_b, x_b = swap(y_b, SUB, 1), swap(x_b, GRP, 1)
    x_a, y_a = swap(x_a, GRP, 0), swap(y_a, SUB, 0)
    return x_a, x_b, y_a, y_b


def copy_sems(count):
    return pltpu.SemaphoreType.DMA((CHUNKS, count))


def local(right_side, conductivity, pinned_cells, coarse_basis, coarse_inverse):
    face = (SRC, CY, CZ)
    block = (CX, CY, CZ)
    tile = (8, 128)
    bases = (VEC, *block)

    def coarse_answer(pieces):
        gathered = exchange(pieces, SUB)
        (partial,) = call(
            coarse_kernel, [(N_GRP, *tile)], [(N_SUB * VEC, 128)], gathered, coarse_inverse
        )
        return exchange(partial, GRP)

    def precondition(pieces, field):
        smoothed, *edges, carried = call(
            prolong_kernel,
            [FIELD, face, face, face, face, tile],
            [bases, FIELD, copy_sems(2)],
            coarse_answer(pieces),
            coarse_basis,
            field,
            scaling,
            keep,
            far=(1, 2),
            limit=PROLONG_LIMIT,
        )
        return smoothed, swap_edges(*edges), carried

    g, s = position()
    ends = (
        *in_order(g, conductivity[-1], conductivity[0]),
        *in_order(s, conductivity[:, -1], conductivity[:, 0]),
    )
    (pieces,) = call(
        restrict_kernel,
        [(N_SUB, *tile)],
        [bases, FIELD, (VEC * 8, 128), copy_sems(2)],
        coarse_basis,
        right_side,
        far=(0, 1),
        limit=FULL_LIMIT,
    )
    scaling, keep, coef, edge = call(
        faces_kernel,
        [block, block, (7, *block), (2, CX, CZ)],
        [],
        conductivity,
        pinned_cells,
        *swap_edges(*ends),
    )
    pieces, scaling, keep, coef, edge = lax.optimization_barrier(
        (pieces, scaling, keep, coef, edge)
    )
    first, edges, _ = precondition(pieces, right_side)
    (inner,) = call(inner_kernel, [FIELD], [], first, coef)
    first_image, pieces = call(
        first_image_kernel,
        [FIELD, (N_SUB, *tile)],
        [FIELD, (VEC * 8 + 128, 128), (128, 128), bases, FIELD, copy_sems(1), copy_sems(2)],
        inner,
        *edges,
        coef,
        edge,
        first,
        coarse_basis,
        right_side,
        far=(8, 9, 10),
        limit=IMAGE_LIMIT,
    )
    second, edges, carried = precondition(pieces, first_image)
    inner, early = call(inner_and_early_kernel, [FIELD, (16, 128)], [], second, coef, carried)
    second_image, pieces = call(
        second_image_kernel,
        [FIELD, (N_GRP, *tile)],
        [FIELD, (256, 128), FIELD, copy_sems(1), copy_sems(1)],
        inner,
        *edges,
        coef,
        edge,
        second,
        first_image,
        far=(8, 9),
        limit=IMAGE_LIMIT,
    )
    (pieces,) = call(relay_kernel, [(N_SUB, *tile)], [], exchange(pieces, GRP))
    return tuple(
        call(
            finish_kernel,
            [FIELD, FIELD],
            [FIELD] * 7 + [copy_sems(5), copy_sems(2)],
            exchange(pieces, SUB),
            carried,
            early,
            first,
            second,
            first_image,
            second_image,
            right_side,
            far=(3, 4, 5, 6, 7, 8, 9),
            limit=FULL_LIMIT,
        )
    )


def solution(mesh):
    split_mesh = Mesh(
        mesh.devices.reshape(2, 4, 4, 4, 2), ("grp_0", "grp_1", "sub_0", "sub_1", "sub_2")
    )
    in_specs = (
        P(None, GRP, SUB, None),
        P(GRP, SUB, None),
        P(GRP, SUB, None),
        P(None, GRP, SUB, None),
        P(None, SUB, GRP),
    )
    out_specs = (P(None, GRP, SUB, None), P(None, GRP, SUB, None))
    return jax.shard_map(
        local, mesh=split_mesh, in_specs=in_specs, out_specs=out_specs, check_vma=False
    )
```
